512 devices in a mesh: section: 8 (over x, core), expert: 64 (over y, z).
Axes of the slice: x: 4, y: 8, z: 8, core: 2. Of those that a mesh axis runs over, the one named last changes fastest.
Arguments:
- states: bfloat16 [8, 2048, 2048], P('section', 'expert'), may hold values from -24 to 24
- incoming: bfloat16 [1, 2048, 2048], P(None, 'expert'), may hold values from -24 to 24
- norm_gain: float32 [8, 2048], P('section'), may hold values from 0.5 to 2
- w_gate_up: bfloat16 [8, 64, 2048, 768], P('section', 'expert'), may hold values from -0.125 to 0.125
- w_down: bfloat16 [8, 64, 384, 2048], P('section', 'expert'), may hold values from -0.15625 to 0.15625
- routes: int32 [2, 8, 2048, 4], P(None, 'section', 'expert'), may hold values from 0 to 15, all different within a row; in each aligned block of 32 rows (0 to 31, 32 to 63, ..., all dimensions but the last counted through in order) at most 10 rows name the same one
- scores: float32 [2, 8, 2048, 4], P(None, 'section', 'expert'), may hold values from 0.05 to 1
Outputs:
- layer_out: bfloat16 [2, 8, 2048, 2048], P(None, 'section', 'expert')
The draws below stay inside these ranges and needn't reach their ends.
Inputs may be any that keep to these rules, and one draw needn't show every extreme that they name: `routes`: in each aligned block of 32 rows (the tokens of one device at one tick and section) no expert is named by more than 10 rows, a bound that some block reaches; a row names 4 different experts.
All inputs are finite; a program needn't handle non-finite values.
Results may differ from the reference program's by a relative error of at most 0.012.
Values may be sent and summed in bfloat16 or wider, within the bound.
No kernel may reach another device: no remote copies, remote signals or barrier semaphores. Data moves between devices by JAX's collectives and lax.ppermute only.
A program may use at most 64 MiB of HBM per device.

```python
import math
import jax
import jax.numpy as jnp
import numpy as np
from jax import lax

D = 2048
FF = 1536
SLICES = 4
TOPK = 4
TICKS = 2
TOK_DEV = 32
HID = 384
EXPERTS = 16
CAP = 10
TOKC = 2048
N_SECTION = 8


def scaled_field(key, shape):
    first, second, third = jax.random.split(key, 3)
    base = jax.random.truncated_normal(first, -4.0, 4.0, shape, jnp.float32)
    row_scale = jnp.exp(jax.random.uniform(second, shape[:-1] + (1,), jnp.float32, math.log(0.3), math.log(3.0)))
    column_scale = jnp.exp(jax.random.uniform(third, (shape[-1],), jnp.float32, math.log(0.5), math.log(2.0)))
    return (base * row_scale * column_scale).astype(jnp.bfloat16)


def draw_states(key, part):
    return scaled_field(jax.random.fold_in(key, 11), (N_SECTION, TOKC, D))


def draw_incoming(key, part):
    return scaled_field(jax.random.fold_in(key, 23), (TICKS - 1, TOKC, D))


def levels(key, shape, cuts, low, high):
    def one(position, blocks):
        draws = jax.random.uniform(jax.random.fold_in(jax.random.fold_in(key, 6), position), (blocks,), jnp.float32, low / len(cuts), high / len(cuts))
        return jnp.repeat(jnp.exp(draws), shape[position] // blocks).reshape((-1,) + (1,) * (len(shape) - position - 1))

    level = one(*cuts[0])
    for cut in cuts[1:]:
        level = level * one(*cut)
    return level


def routed_block(own_key, own, number, rows, number_of, top, bound, skew):
    sequence = jax.random.permutation(own_key, number_of)
    heavy_load, ordinary = portions_of(number_of, rows * top, bound, skew, True), portions_of(number_of, rows * top, bound, skew, False)
    places = jnp.arange(number_of)

    def named(lengths, rotation):
        used = int((lengths > 0).sum())
        fixed = max(1, used // 4)
        moved = fixed + (places - fixed + rotation * (used - fixed)) % max(1, number_of - fixed)
        return jnp.zeros((number_of,), jnp.int32).at[sequence[jnp.where(places < fixed, places, moved)]].set(jnp.asarray(lengths, jnp.int32))

    lengths = jnp.where(number % 4 == 0, named(heavy_load, number // 4), named(ordinary, number - number // 4 - 1))
    mixed = jax.random.permutation(jax.random.fold_in(own, 3), number_of)
    giver, taker = mixed[0:number_of // 2 * 2:2], mixed[1:number_of // 2 * 2:2]
    slack = jnp.minimum(lengths[giver] - 1, bound - lengths[taker]) // 2
    slack = jnp.where((giver == sequence[0]) | (taker == sequence[0]) | (lengths[taker] == 0), 0, jnp.maximum(slack, 0))
    moved = jax.random.randint(jax.random.fold_in(own, 4), (number_of // 2,), 0, 1 << 20) % (slack + 1)
    lengths = lengths.at[giver].add(-moved).at[taker].add(moved)
    labels = jnp.searchsorted(jnp.cumsum(lengths), jnp.arange(rows * top), side="right").astype(jnp.int32)
    table = labels.reshape(top, rows).T
    table = table[jax.random.permutation(jax.random.fold_in(own, 1), rows)]
    rotation = jax.random.randint(jax.random.fold_in(own, 2), (rows, 1), 0, top)
    return jnp.take_along_axis(table, (jnp.arange(top)[None, :] + rotation) % top, axis=1)


def portions_of(amount, total, most, lean, full):
    weights = [(1 << 20) // math.isqrt(standing ** lean) + 1 for standing in range(1, amount + 1)]
    largest = most if full else min(most, max(-(-total // amount), total * weights[0] // sum(weights)))
    least = 1 if total - largest >= amount - 1 else 0
    given, rest = [largest] + [least] * (amount - 1), total - largest - least * (amount - 1)
    while rest > 0:
        candidates = [i for i in range(1, amount) if given[i] < largest] or [i for i in range(1, amount) if given[i] < most]
        whole, remaining = sum([weights[i] for i in candidates]), rest
        for i in candidates:
            addition = min(most - given[i], max(1, remaining * weights[i] // whole), rest)
            given[i] = given[i] + addition
            rest = rest - addition
    return np.array(given)


def gaussian(stream_key, extent, scale, bound, cuts=(), kind=jnp.bfloat16):
    loudness = levels(stream_key, extent, cuts, -0.22, 0.18) if cuts else 1.0
    values = jax.random.normal(stream_key, extent, jnp.float32) * scale * loudness
    return jnp.minimum(jnp.maximum(values, -bound), bound).astype(kind)


def setup_inputs(seed: int = 0) -> dict:
    splits = jax.random.split(jax.random.key(seed), 8)
    states = draw_states(jax.random.fold_in(splits[7], 71), 0)
    incoming = draw_incoming(jax.random.fold_in(splits[7], 71), 0)
    norm_gain = jnp.clip(jnp.exp(math.log(2.0) - 1.3862944 * jax.random.uniform(splits[2], (N_SECTION, D), jnp.float32) ** levels(splits[2], (N_SECTION, D), ((0, 8),), -0.2, 0.2)), 0.5, 2.0)
    w_gate_up = gaussian(splits[3], (N_SECTION, EXPERTS * SLICES, D, 2 * HID), D ** -0.5, 0.125, ((0, 8), (1, 64)))
    w_down = gaussian(splits[4], (N_SECTION, EXPERTS * SLICES, HID, D), FF ** -0.5, 0.15625, ((0, 8), (1, 64)))
    routes_keys = jax.random.split(jax.random.fold_in(splits[5], 1), TICKS * N_SECTION * TOKC // TOK_DEV)
    routes_turns = jax.random.permutation(jax.random.fold_in(splits[5], 3), TICKS * N_SECTION * TOKC // TOK_DEV)
    routes = jax.vmap(lambda own, number: routed_block(jax.random.fold_in(splits[5], 2), own, number, TOK_DEV, EXPERTS, TOPK, CAP, 2))(routes_keys, routes_turns).reshape((TICKS, N_SECTION, TOKC, TOPK))
    scores = jnp.clip(jnp.exp(math.log(1.0) - 2.9957323 * jax.random.uniform(splits[6], (TICKS, N_SECTION, TOKC, TOPK), jnp.float32) ** levels(splits[6], (TICKS, N_SECTION, TOKC, TOPK), ((1, 8), (2, 64)), -0.2, 0.2)), 0.05, 1.0)
    return {"states": states, "incoming": incoming, "norm_gain": norm_gain, "w_gate_up": w_gate_up, "w_down": w_down, "routes": routes, "scores": scores}


epsilon = 1e-06

def section_layer(current, gain_values, gate_up_weights, down_weights, chosen_routes, router_scores):
    blocks_count = TOKC // TOK_DEV
    values = current.astype(jnp.float32)
    mean_square = lax.optimization_barrier(jnp.mean(values * values, axis=-1, keepdims=True))
    normed = (values * lax.rsqrt(mean_square + epsilon) * gain_values).astype(jnp.bfloat16)
    chosen = chosen_routes.reshape(blocks_count, TOK_DEV * TOPK).astype(jnp.int32)
    onehot = (chosen[:, :, None] == jnp.arange(EXPERTS, dtype=jnp.int32)[None, None, :]).astype(jnp.int32)
    slot_index = lax.optimization_barrier(jnp.sum((jnp.cumsum(onehot, axis=1) - onehot) * onehot, axis=2)).astype(jnp.int32)
    token_index = (jnp.arange(TOK_DEV * TOPK, dtype=jnp.int32) // TOPK).astype(jnp.int32)
    source_index = jnp.arange(blocks_count, dtype=jnp.int32)[:, None]
    pieces = normed.reshape(blocks_count, TOK_DEV, D)
    buffers = jnp.zeros((EXPERTS, blocks_count, CAP, D), jnp.bfloat16)
    buffers = buffers.at[chosen, source_index, slot_index].set(pieces[source_index, token_index[None, :]])

    def run_expert(operands):
        rows_in, gate_up, down = operands
        projected = jnp.einsum('md,jdh->jmh', rows_in.astype(jnp.float32), gate_up.astype(jnp.float32))
        hidden = (jax.nn.silu(projected[..., :HID]) * projected[..., HID:]).astype(jnp.bfloat16)
        partial_value = jnp.einsum('jmh,jhd->jmd', hidden.astype(jnp.float32), down.astype(jnp.float32))
        return lax.optimization_barrier(jnp.sum(partial_value, axis=0)).astype(jnp.bfloat16)
    expert_out = lax.map(run_expert, (buffers.reshape(EXPERTS, blocks_count * CAP, D), gate_up_weights.reshape(EXPERTS, SLICES, D, 2 * HID), down_weights.reshape(EXPERTS, SLICES, HID, D)))
    expert_out = expert_out.reshape(EXPERTS, blocks_count, CAP, D)
    gathered_rows = expert_out[chosen, source_index, slot_index]
    weight = router_scores / lax.optimization_barrier(jnp.sum(router_scores, axis=-1, keepdims=True))
    branch = lax.optimization_barrier(jnp.sum(weight.reshape(blocks_count, TOK_DEV, TOPK, 1) * gathered_rows.reshape(blocks_count, TOK_DEV, TOPK, D).astype(jnp.float32), axis=2))
    result = current.reshape(blocks_count, TOK_DEV, D).astype(jnp.float32) + branch
    return result.astype(jnp.bfloat16).reshape(TOKC, D)

def reference(states, incoming, norm_gain, w_gate_up, w_down, routes, scores):
    current = [section_layer(states[section_number], norm_gain[section_number], w_gate_up[section_number], w_down[section_number], routes[0, section_number], scores[0, section_number]) for section_number in range(N_SECTION)]
    outputs = [jnp.stack(current)]
    for tick_index in range(1, TICKS):
        inputs = [incoming[tick_index - 1]] + current[:-1]
        current = [section_layer(inputs[section_number], norm_gain[section_number], w_gate_up[section_number], w_down[section_number], routes[tick_index, section_number], scores[tick_index, section_number]) for section_number in range(N_SECTION)]
        outputs.append(jnp.stack(current))
    return jnp.stack(outputs)
```

```python
import jax
import jax.numpy as jnp
from jax import lax
from jax.sharding import PartitionSpec as P

SLICES = 4
TOPK = 4
TICKS = 2
LANES = 128
ROWS = 8
SHARE = 2


epsilon = 1e-06


def shifted(x, axis, by):
    length = lax.axis_size(axis)
    pairs = [(i, i + by) for i in range(length) if 0 <= i + by < length]
    return lax.ppermute(x, axis, pairs)


def normalize(current, gain_values):
    values = current.astype(jnp.float32)
    mean_square = jnp.mean(values * values, axis=-1, keepdims=True)
    return (values * lax.rsqrt(mean_square + epsilon) * gain_values).astype(jnp.bfloat16)


def to_tiles(rows, groups):
    r = rows.shape[0] // groups
    blocks = rows.shape[1] // LANES
    return rows.reshape(groups, r, blocks, LANES).transpose(0, 2, 1, 3).reshape(groups, blocks * r, LANES)


def from_tiles(tiles, r):
    groups, _, _ = tiles.shape
    blocks = tiles.shape[1] // r
    return tiles.reshape(groups, blocks, r, LANES).transpose(0, 2, 1, 3).reshape(groups * r, blocks * LANES)


def slots_of(chosen, expert_count):
    onehot = (chosen[:, None] == jnp.arange(expert_count, dtype=jnp.int32)[None, :]).astype(jnp.int32)
    return jnp.sum((jnp.cumsum(onehot, axis=0) - onehot) * onehot, axis=1)


def exchange(x):
    length = lax.axis_size("expert")
    groups = [list(range(first, length, SHARE)) for first in range(SHARE)]
    return lax.all_to_all(x, "expert", split_axis=0, concat_axis=0, tiled=True, axis_index_groups=groups)


def swapped(x):
    length = lax.axis_size("expert")
    return lax.ppermute(x, "expert", [(i, i ^ 1) for i in range(length)])


def per_device(states, incoming, norm_gain, w_gate_up, w_down, routes, scores):
    group = lax.axis_size("expert") // SHARE
    copies = SLICES // SHARE
    expert_count = group // copies
    tokens = states.shape[1]
    capacity = min(tokens, max(2, 5 * tokens * TOPK // (4 * expert_count)))
    parts = []
    low = 0
    while low < capacity:
        high = min(low + ROWS, capacity)
        parts.append((low, high))
        low = high
    hidden_width = w_down.shape[2]
    section_index = lax.axis_index("section")
    gate_up_weights = [w_gate_up[0, 0], swapped(w_gate_up[0, 0])]
    down_weights = [w_down[0, 0], swapped(w_down[0, 0])]
    gain_values = norm_gain[0]
    plans = []
    for tick_index in range(TICKS):
        chosen = routes[tick_index, 0].reshape(-1)
        slot = slots_of(chosen, expert_count)
        router_scores = scores[tick_index, 0]
        weight = (router_scores / jnp.sum(router_scores, axis=-1, keepdims=True)).reshape(-1)
        plan = []
        for low, high in parts:
            size = high - low
            inside = (slot >= low) & (slot < high)
            target = jnp.where(inside, chosen * size + slot - low, -1)
            matches = jnp.arange(expert_count * size, dtype=jnp.int32)[:, None] == target[None, :]
            matches = matches.reshape(expert_count * size, tokens, TOPK)
            picker = jnp.any(matches, axis=2).astype(jnp.bfloat16)
            weights = jnp.sum(jnp.where(matches, weight.reshape(1, tokens, TOPK), 0.0), axis=2)
            upper = weights.astype(jnp.bfloat16)
            lower = (weights - upper.astype(jnp.float32)).astype(jnp.bfloat16)
            plan.append((picker, upper, lower))
        plans.append(plan)
    current = states[0]
    outputs = []
    for tick_index in range(TICKS):
        plan = plans[tick_index]
        normed = normalize(current, gain_values)
        sent = []
        for (low, high), (picker, _, _) in zip(parts, plan):
            packed = jnp.dot(picker, normed, preferred_element_type=jnp.float32).astype(jnp.bfloat16)
            sent.append(to_tiles(packed, expert_count))
        received = exchange(jnp.repeat(jnp.concatenate(sent, axis=1), copies, axis=0))
        at = [sum(p.shape[1] for p in sent[:i]) for i in range(len(sent) + 1)]
        rows_in = [from_tiles(received[:, at[i]:at[i + 1]], high - low) for i, (low, high) in enumerate(parts)]
        rows_in = jnp.concatenate(rows_in, axis=0)
        partial_value = 0.0
        for gate_up, down in zip(gate_up_weights, down_weights):
            projected = jnp.dot(rows_in, gate_up, preferred_element_type=jnp.float32)
            hidden = (jax.nn.silu(projected[:, :hidden_width]) * projected[:, hidden_width:]).astype(jnp.bfloat16)
            partial_value = partial_value + jnp.dot(hidden, down, preferred_element_type=jnp.float32)
        partial_value = partial_value.astype(jnp.bfloat16)
        split = [partial_value[group * low:group * high] for low, high in parts]
        back = exchange(jnp.concatenate([to_tiles(piece, group) for piece in split], axis=1))
        returned = [back[:, at[i]:at[i + 1]] for i in range(len(sent))]
        branch = 0.0
        for (low, high), piece, (_, upper, lower) in zip(parts, returned, plan):
            summed = jnp.sum(piece.reshape(expert_count, copies, piece.shape[1], LANES).astype(jnp.float32), axis=1)
            table = from_tiles(summed.astype(jnp.bfloat16), high - low)
            contract = (((0,), (0,)), ((), ()))
            branch = branch + lax.dot_general(upper, table, contract, preferred_element_type=jnp.float32)
            branch = branch + lax.dot_general(lower, table, contract, preferred_element_type=jnp.float32)
        result = (current.astype(jnp.float32) + branch).astype(jnp.bfloat16)
        outputs.append(result)
        if tick_index + 1 < TICKS:
            passed = shifted(result, "section", 1)
            current = jnp.where(section_index == 0, incoming[tick_index], passed)
    return jnp.stack(outputs)[:, None]


def solution(mesh):
    return jax.shard_map(
        per_device,
        mesh=mesh,
        in_specs=(
            P("section", "expert", None),
            P(None, "expert", None),
            P("section", None),
            P("section", "expert", None, None),
            P("section", "expert", None, None),
            P(None, "section", "expert", None),
            P(None, "section", "expert", None),
        ),
        out_specs=P(None, "section", "expert", None),
        check_vma=False,
    )
```

```python
import jax
import jax.numpy as jnp
from jax import lax
from jax.sharding import PartitionSpec as P

SLICES = 4
TOPK = 4
TICKS = 2
LANES = 128
ROWS = 8
COLUMNS = 8
SHARE = 2


epsilon = 1e-06


def shifted(x, axis, by):
    length = lax.axis_size(axis)
    pairs = [(i, i + by) for i in range(length) if 0 <= i + by < length]
    return lax.ppermute(x, axis, pairs)


def normalize(current, gain_values):
    values = current.astype(jnp.float32)
    mean_square = jnp.mean(values * values, axis=-1, keepdims=True)
    return (values * lax.rsqrt(mean_square + epsilon) * gain_values).astype(jnp.bfloat16)


def to_tiles(rows, groups):
    r = rows.shape[0] // groups
    blocks = rows.shape[1] // LANES
    return rows.reshape(groups, r, blocks, LANES).transpose(0, 2, 1, 3).reshape(groups, blocks * r, LANES)


def from_tiles(tiles, r):
    groups, _, _ = tiles.shape
    blocks = tiles.shape[1] // r
    return tiles.reshape(groups, blocks, r, LANES).transpose(0, 2, 1, 3).reshape(groups * r, blocks * LANES)


def slots_of(chosen, expert_count):
    onehot = (chosen[:, None] == jnp.arange(expert_count, dtype=jnp.int32)[None, :]).astype(jnp.int32)
    return jnp.sum((jnp.cumsum(onehot, axis=0) - onehot) * onehot, axis=1)


def exchange(x):
    length = lax.axis_size("expert")
    groups = [list(range(first, length, SHARE)) for first in range(SHARE)]
    return lax.all_to_all(x, "expert", split_axis=0, concat_axis=0, tiled=True, axis_index_groups=groups)


def same_side(x):
    length = lax.axis_size("expert")
    pieces = [x]
    for by in range(SHARE, COLUMNS, SHARE):
        pairs = [(i, i // COLUMNS * COLUMNS + (i + by) % COLUMNS) for i in range(length)]
        pieces.append(lax.ppermute(x, "expert", pairs))
    return jnp.stack(pieces)


def exchange_rows(x):
    length = lax.axis_size("expert")
    groups = [list(range(first, length, COLUMNS)) for first in range(COLUMNS)]
    return lax.all_to_all(x, "expert", split_axis=0, concat_axis=0, tiled=True, axis_index_groups=groups)


def swapped(x):
    length = lax.axis_size("expert")
    return lax.ppermute(x, "expert", [(i, i ^ 1) for i in range(length)])


def first_dispatch(normed, chosen, parts, column, expert_count, swapped_first):
    tokens, width = normed.shape
    rows_of_chips = lax.axis_size("expert") // COLUMNS
    halves = expert_count // rows_of_chips
    sources = COLUMNS // SHARE
    slot = slots_of(chosen.reshape(-1), expert_count).reshape(tokens, TOPK)
    named = chosen[:, :, None] == jnp.arange(expert_count, dtype=jnp.int32)[None, None, :]
    slot_at = jnp.sum(jnp.where(named, slot[:, :, None] + 1, 0), axis=1)
    slot_at = jnp.pad(slot_at, ((0, 0), (0, LANES - expert_count))).astype(jnp.bfloat16)
    everyone = same_side(jnp.concatenate([normed, slot_at], axis=1))
    mine = column // SHARE
    position = (mine - jnp.arange(sources, dtype=jnp.int32)) % sources
    origin = jnp.arange(sources, dtype=jnp.int32)[:, None] == position[None, :]
    slots = everyone[:, :, width:width + expert_count].astype(jnp.int32) - 1
    slots = slots.reshape(sources, tokens, rows_of_chips, halves)
    half = column // (COLUMNS // halves)
    slots = jnp.sum(jnp.where(jnp.arange(halves, dtype=jnp.int32) == half, slots, 0), axis=3)
    pieces = []
    for low, high in parts:
        place = jnp.arange(low, high, dtype=jnp.int32)
        match = slots.transpose(2, 0, 1)[:, None, None, :, :] == place[None, None, :, None, None]
        match = match & origin[None, :, None, :, None]
        pieces.append(match.reshape(rows_of_chips, sources * (high - low), sources * tokens))
    picker = jnp.concatenate(pieces, axis=1).astype(jnp.bfloat16)
    count = picker.shape[1]
    flat = everyone[:, :, :width].reshape(sources * tokens, width)
    packed = jnp.dot(picker.reshape(rows_of_chips * count, sources * tokens), flat, preferred_element_type=jnp.float32)
    packed = packed.astype(jnp.bfloat16).reshape(rows_of_chips, count, width)
    packed, _ = lax.optimization_barrier((packed, swapped_first))
    received = exchange_rows(packed)
    rows_in = []
    first = 0
    for low, high in parts:
        size = sources * (high - low)
        rows_in.append(received[:, first:first + size].reshape(rows_of_chips * size, width))
        first += size
    return jnp.concatenate(rows_in, axis=0)


def per_device(states, incoming, norm_gain, w_gate_up, w_down, routes, scores):
    group = lax.axis_size("expert") // SHARE
    copies = SLICES // SHARE
    expert_count = group // copies
    tokens = states.shape[1]
    capacity = min(tokens, max(2, 5 * tokens * TOPK // (4 * expert_count)))
    parts = []
    low = 0
    while low < capacity:
        high = min(low + ROWS, capacity)
        parts.append((low, high))
        low = high
    hidden_width = w_down.shape[2]
    column = lax.axis_index("expert") % COLUMNS
    section_index = lax.axis_index("section")
    gate_up_weights = [w_gate_up[0, 0], swapped(w_gate_up[0, 0])]
    down_weights = [w_down[0, 0], swapped(w_down[0, 0])]
    gain_values = norm_gain[0]
    plans = []
    for tick_index in range(TICKS):
        chosen = routes[tick_index, 0].reshape(-1)
        slot = slots_of(chosen, expert_count)
        router_scores = scores[tick_index, 0]
        weight = (router_scores / jnp.sum(router_scores, axis=-1, keepdims=True)).reshape(-1)
        plan = []
        for low, high in parts:
            size = high - low
            inside = (slot >= low) & (slot < high)
            target = jnp.where(inside, chosen * size + slot - low, -1)
            matches = jnp.arange(expert_count * size, dtype=jnp.int32)[:, None] == target[None, :]
            matches = matches.reshape(expert_count * size, tokens, TOPK)
            picker = jnp.any(matches, axis=2).astype(jnp.bfloat16)
            weights = jnp.sum(jnp.where(matches, weight.reshape(1, tokens, TOPK), 0.0), axis=2)
            upper = weights.astype(jnp.bfloat16)
            lower = (weights - upper.astype(jnp.float32)).astype(jnp.bfloat16)
            plan.append((picker, upper, lower))
        plans.append(plan)
    current = states[0]
    outputs = []
    for tick_index in range(TICKS):
        plan = plans[tick_index]
        normed = normalize(current, gain_values)
        at = [0]
        for low, high in parts:
            at.append(at[-1] + (high - low) * normed.shape[1] // LANES)
        if tick_index == 0:
            rows_in = first_dispatch(normed, routes[0, 0], parts, column, expert_count, gate_up_weights[1])
        else:
            sent = []
            for (low, high), (picker, _, _) in zip(parts, plan):
                packed = jnp.dot(picker, normed, preferred_element_type=jnp.float32).astype(jnp.bfloat16)
                sent.append(to_tiles(packed, expert_count))
            received = exchange(jnp.repeat(jnp.concatenate(sent, axis=1), copies, axis=0))
            rows_in = [from_tiles(received[:, at[i]:at[i + 1]], high - low) for i, (low, high) in enumerate(parts)]
            rows_in = jnp.concatenate(rows_in, axis=0)
        partial_value = 0.0
        for gate_up, down in zip(gate_up_weights, down_weights):
            projected = jnp.dot(rows_in, gate_up, preferred_element_type=jnp.float32)
            hidden = (jax.nn.silu(projected[:, :hidden_width]) * projected[:, hidden_width:]).astype(jnp.bfloat16)
            partial_value = partial_value + jnp.dot(hidden, down, preferred_element_type=jnp.float32)
        partial_value = partial_value.astype(jnp.bfloat16)
        split = [partial_value[group * low:group * high] for low, high in parts]
        back = exchange(jnp.concatenate([to_tiles(piece, group) for piece in split], axis=1))
        returned = [back[:, at[i]:at[i + 1]] for i in range(len(parts))]
        branch = 0.0
        for (low, high), piece, (_, upper, lower) in zip(parts, returned, plan):
            summed = jnp.sum(piece.reshape(expert_count, copies, piece.shape[1], LANES).astype(jnp.float32), axis=1)
            table = from_tiles(summed.astype(jnp.bfloat16), high - low)
            contract = (((0,), (0,)), ((), ()))
            branch = branch + lax.dot_general(upper, table, contract, preferred_element_type=jnp.float32)
            branch = branch + lax.dot_general(lower, table, contract, preferred_element_type=jnp.float32)
        result = (current.astype(jnp.float32) + branch).astype(jnp.bfloat16)
        outputs.append(result)
        if tick_index + 1 < TICKS:
            passed = shifted(result, "section", 1)
            current = jnp.where(section_index == 0, incoming[tick_index], passed)
    return jnp.stack(outputs)[:, None]


def solution(mesh):
    return jax.shard_map(
        per_device,
        mesh=mesh,
        in_specs=(
            P("section", "expert", None),
            P(None, "expert", None),
            P("section", None),
            P("section", "expert", None, None),
            P("section", "expert", None, None),
            P(None, "section", "expert", None),
            P(None, "section", "expert", None),
        ),
        out_specs=P(None, "section", "expert", None),
        check_vma=False,
    )
```

```python
import jax
import jax.numpy as jnp
from jax import lax
from jax.sharding import PartitionSpec as P

SLICES = 4
TOPK = 4
TICKS = 2
LANES = 128
ROWS = 8
COLUMNS = 8
SHARE = 2


epsilon = 1e-06


def shifted(x, axis, by):
    length = lax.axis_size(axis)
    pairs = [(i, i + by) for i in range(length) if 0 <= i + by < length]
    return lax.ppermute(x, axis, pairs)


def normalize(current, gain_values):
    values = current.astype(jnp.float32)
    mean_square = jnp.mean(values * values, axis=-1, keepdims=True)
    return (values * lax.rsqrt(mean_square + epsilon) * gain_values).astype(jnp.bfloat16)


def to_tiles(rows, groups):
    r = rows.shape[0] // groups
    blocks = rows.shape[1] // LANES
    return rows.reshape(groups, r, blocks, LANES).transpose(0, 2, 1, 3).reshape(groups, blocks * r, LANES)


def from_tiles(tiles, r):
    groups, _, _ = tiles.shape
    blocks = tiles.shape[1] // r
    return tiles.reshape(groups, blocks, r, LANES).transpose(0, 2, 1, 3).reshape(groups * r, blocks * LANES)


def slots_of(chosen, expert_count):
    onehot = (chosen[:, None] == jnp.arange(expert_count, dtype=jnp.int32)[None, :]).astype(jnp.int32)
    return jnp.sum((jnp.cumsum(onehot, axis=0) - onehot) * onehot, axis=1)


def exchange(x):
    length = lax.axis_size("expert")
    groups = [list(range(first, length, SHARE)) for first in range(SHARE)]
    return lax.all_to_all(x, "expert", split_axis=0, concat_axis=0, tiled=True, axis_index_groups=groups)


def same_side(x):
    length = lax.axis_size("expert")
    pieces = [x]
    for by in range(SHARE, COLUMNS, SHARE):
        pairs = [(i, i // COLUMNS * COLUMNS + (i + by) % COLUMNS) for i in range(length)]
        pieces.append(lax.ppermute(x, "expert", pairs))
    return jnp.stack(pieces)


def exchange_rows(x):
    length = lax.axis_size("expert")
    groups = [list(range(first, length, COLUMNS)) for first in range(COLUMNS)]
    return lax.all_to_all(x, "expert", split_axis=0, concat_axis=0, tiled=True, axis_index_groups=groups)


def swapped(x):
    length = lax.axis_size("expert")
    return lax.ppermute(x, "expert", [(i, i ^ 1) for i in range(length)])


def gated(rows, weights):
    half = weights.shape[1] // 2
    projected = jnp.dot(rows, weights, preferred_element_type=jnp.float32)
    return (jax.nn.silu(projected[:, :half]) * projected[:, half:]).astype(jnp.bfloat16)


def first_dispatch(normed, chosen, parts, column, expert_count, swapped_first):
    tokens, width = normed.shape
    rows_of_chips = lax.axis_size("expert") // COLUMNS
    halves = expert_count // rows_of_chips
    sources = COLUMNS // SHARE
    slot = slots_of(chosen.reshape(-1), expert_count).reshape(tokens, TOPK)
    named = chosen[:, :, None] == jnp.arange(expert_count, dtype=jnp.int32)[None, None, :]
    slot_at = jnp.sum(jnp.where(named, slot[:, :, None] + 1, 0), axis=1)
    slot_at = jnp.pad(slot_at, ((0, 0), (0, LANES - expert_count))).astype(jnp.bfloat16)
    everyone = same_side(jnp.concatenate([normed, slot_at], axis=1))
    everyone, _ = lax.optimization_barrier((everyone, swapped_first))
    mine = column // SHARE
    position = (mine - jnp.arange(sources, dtype=jnp.int32)) % sources
    origin = jnp.arange(sources, dtype=jnp.int32)[:, None] == position[None, :]
    slots = everyone[:, :, width:width + expert_count].astype(jnp.int32) - 1
    slots = slots.reshape(sources, tokens, rows_of_chips, halves)
    half = column // (COLUMNS // halves)
    slots = jnp.sum(jnp.where(jnp.arange(halves, dtype=jnp.int32) == half, slots, 0), axis=3)
    pieces = []
    for low, high in parts:
        place = jnp.arange(low, high, dtype=jnp.int32)
        match = slots.transpose(2, 0, 1)[:, None, None, :, :] == place[None, None, :, None, None]
        match = match & origin[None, :, None, :, None]
        pieces.append(match.reshape(rows_of_chips, sources * (high - low), sources * tokens))
    picker = jnp.concatenate(pieces, axis=1).astype(jnp.bfloat16)
    count = picker.shape[1]
    flat = everyone[:, :, :width].reshape(sources * tokens, width)
    packed = jnp.dot(picker.reshape(rows_of_chips * count, sources * tokens), flat, preferred_element_type=jnp.float32)
    packed = packed.astype(jnp.bfloat16).reshape(rows_of_chips, count, width)
    received = exchange_rows(packed)
    rows_in = []
    first = 0
    for low, high in parts:
        size = sources * (high - low)
        rows_in.append(received[:, first:first + size].reshape(rows_of_chips * size, width))
        first += size
    return jnp.concatenate(rows_in, axis=0)


def per_device(states, incoming, norm_gain, w_gate_up, w_down, routes, scores):
    group = lax.axis_size("expert") // SHARE
    copies = SLICES // SHARE
    expert_count = group // copies
    tokens = states.shape[1]
    capacity = min(tokens, max(2, 5 * tokens * TOPK // (4 * expert_count)))
    parts = []
    low = 0
    while low < capacity:
        high = min(low + ROWS, capacity)
        parts.append((low, high))
        low = high
    column = lax.axis_index("expert") % COLUMNS
    section_index = lax.axis_index("section")
    gate_up_own, down_own = w_gate_up[0, 0], w_down[0, 0]
    wide = gate_up_own.shape[1]
    down_last = swapped(down_own[:, wide:])
    joined = swapped(jnp.concatenate([gate_up_own, down_own[:, :wide]], axis=0))
    gate_up_other, down_first = joined[:gate_up_own.shape[0]], joined[gate_up_own.shape[0]:]
    gain_values = norm_gain[0]
    plans = []
    for tick_index in range(TICKS):
        chosen = routes[tick_index, 0].reshape(-1)
        slot = slots_of(chosen, expert_count)
        router_scores = scores[tick_index, 0]
        weight = (router_scores / jnp.sum(router_scores, axis=-1, keepdims=True)).reshape(-1)
        plan = []
        for low, high in parts:
            size = high - low
            inside = (slot >= low) & (slot < high)
            target = jnp.where(inside, chosen * size + slot - low, -1)
            matches = jnp.arange(expert_count * size, dtype=jnp.int32)[:, None] == target[None, :]
            matches = matches.reshape(expert_count * size, tokens, TOPK)
            picker = jnp.any(matches, axis=2).astype(jnp.bfloat16)
            weights = jnp.sum(jnp.where(matches, weight.reshape(1, tokens, TOPK), 0.0), axis=2)
            upper = weights.astype(jnp.bfloat16)
            lower = (weights - upper.astype(jnp.float32)).astype(jnp.bfloat16)
            plan.append((picker, upper, lower))
        plans.append(plan)
    current = states[0]
    outputs = []
    for tick_index in range(TICKS):
        plan = plans[tick_index]
        normed = normalize(current, gain_values)
        at = [0]
        for low, high in parts:
            at.append(at[-1] + (high - low) * normed.shape[1] // LANES)
        if tick_index == 0:
            rows_in = first_dispatch(normed, routes[0, 0], parts, column, expert_count, down_last)
        else:
            sent = []
            for (low, high), (picker, _, _) in zip(parts, plan):
                packed = jnp.dot(picker, normed, preferred_element_type=jnp.float32).astype(jnp.bfloat16)
                sent.append(to_tiles(packed, expert_count))
            received = exchange(jnp.repeat(jnp.concatenate(sent, axis=1), copies, axis=0))
            rows_in = [from_tiles(received[:, at[i]:at[i + 1]], high - low) for i, (low, high) in enumerate(parts)]
            rows_in = jnp.concatenate(rows_in, axis=0)
        hidden_own = gated(rows_in, gate_up_own)
        hidden_other = gated(rows_in, gate_up_other)
        down_other = jnp.concatenate([down_first, down_last], axis=1)
        partial_value = jnp.dot(hidden_own, down_own, preferred_element_type=jnp.float32)
        partial_value = partial_value + jnp.dot(hidden_other, down_other, preferred_element_type=jnp.float32)
        partial_value = partial_value.astype(jnp.bfloat16)
        split = [partial_value[group * low:group * high] for low, high in parts]
        back = exchange(jnp.concatenate([to_tiles(piece, group) for piece in split], axis=1))
        returned = [back[:, at[i]:at[i + 1]] for i in range(len(parts))]
        branch = 0.0
        for (low, high), piece, (_, upper, lower) in zip(parts, returned, plan):
            summed = jnp.sum(piece.reshape(expert_count, copies, piece.shape[1], LANES).astype(jnp.float32), axis=1)
            table = from_tiles(summed.astype(jnp.bfloat16), high - low)
            contract = (((0,), (0,)), ((), ()))
            branch = branch + lax.dot_general(upper, table, contract, preferred_element_type=jnp.float32)
            branch = branch + lax.dot_general(lower, table, contract, preferred_element_type=jnp.float32)
        result = (current.astype(jnp.float32) + branch).astype(jnp.bfloat16)
        outputs.append(result)
        if tick_index + 1 < TICKS:
            passed = shifted(result, "section", 1)
            current = jnp.where(section_index == 0, incoming[tick_index], passed)
    return jnp.stack(outputs)[:, None]


def solution(mesh):
    return jax.shard_map(
        per_device,
        mesh=mesh,
        in_specs=(
            P("section", "expert", None),
            P(None, "expert", None),
            P("section", None),
            P("section", "expert", None, None),
            P("section", "expert", None, None),
            P(None, "section", "expert", None),
            P(None, "section", "expert", None),
        ),
        out_specs=P(None, "section", "expert", None),
        check_vma=False,
    )
```

```python
import jax
import jax.numpy as jnp
from jax import lax
from jax.sharding import PartitionSpec as P

SLICES = 4
TOPK = 4
TICKS = 2
LANES = 128
ROWS = 8
COLUMNS = 8
SHARE = 2


epsilon = 1e-06


def shifted(x, axis, by):
    length = lax.axis_size(axis)
    pairs = [(i, i + by) for i in range(length) if 0 <= i + by < length]
    return lax.ppermute(x, axis, pairs)


def normalize(current, gain_values):
    values = current.astype(jnp.float32)
    mean_square = jnp.mean(values * values, axis=-1, keepdims=True)
    return (values * lax.rsqrt(mean_square + epsilon) * gain_values).astype(jnp.bfloat16)


def to_tiles(rows, groups):
    r = rows.shape[0] // groups
    blocks = rows.shape[1] // LANES
    return rows.reshape(groups, r, blocks, LANES).transpose(0, 2, 1, 3).reshape(groups, blocks * r, LANES)


def from_tiles(tiles, r):
    groups, _, _ = tiles.shape
    blocks = tiles.shape[1] // r
    return tiles.reshape(groups, blocks, r, LANES).transpose(0, 2, 1, 3).reshape(groups * r, blocks * LANES)


def slots_of(chosen, expert_count):
    onehot = (chosen[:, None] == jnp.arange(expert_count, dtype=jnp.int32)[None, :]).astype(jnp.int32)
    return jnp.sum((jnp.cumsum(onehot, axis=0) - onehot) * onehot, axis=1)


def exchange(x):
    length = lax.axis_size("expert")
    groups = [list(range(first, length, SHARE)) for first in range(SHARE)]
    return lax.all_to_all(x, "expert", split_axis=0, concat_axis=0, tiled=True, axis_index_groups=groups)


def same_side(x):
    length = lax.axis_size("expert")
    pieces = [x]
    for by in range(SHARE, COLUMNS, SHARE):
        pairs = [(i, i // COLUMNS * COLUMNS + (i + by) % COLUMNS) for i in range(length)]
        pieces.append(lax.ppermute(x, "expert", pairs))
    return jnp.stack(pieces)


def exchange_rows(x):
    length = lax.axis_size("expert")
    groups = [list(range(first, length, COLUMNS)) for first in range(COLUMNS)]
    return lax.all_to_all(x, "expert", split_axis=0, concat_axis=0, tiled=True, axis_index_groups=groups)


def swapped(x):
    length = lax.axis_size("expert")
    return lax.ppermute(x, "expert", [(i, i ^ 1) for i in range(length)])


def gated(rows, weights):
    half = weights.shape[1] // 2
    projected = jnp.dot(rows, weights, preferred_element_type=jnp.float32)
    return (jax.nn.silu(projected[:, :half]) * projected[:, half:]).astype(jnp.bfloat16)


def first_dispatch(normed, chosen, parts, column, expert_count, swapped_first):
    tokens, width = normed.shape
    rows_of_chips = lax.axis_size("expert") // COLUMNS
    halves = expert_count // rows_of_chips
    sources = COLUMNS // SHARE
    slot = slots_of(chosen.reshape(-1), expert_count).reshape(tokens, TOPK)
    named = chosen[:, :, None] == jnp.arange(expert_count, dtype=jnp.int32)[None, None, :]
    slot_at = jnp.sum(jnp.where(named, slot[:, :, None] + 1, 0), axis=1)
    slot_at = jnp.pad(slot_at, ((0, 0), (0, LANES - expert_count))).astype(jnp.bfloat16)
    everyone = same_side(jnp.concatenate([normed, slot_at], axis=1))
    everyone, _ = lax.optimization_barrier((everyone, swapped_first))
    mine = column // SHARE
    position = (mine - jnp.arange(sources, dtype=jnp.int32)) % sources
    origin = jnp.arange(sources, dtype=jnp.int32)[:, None] == position[None, :]
    slots = everyone[:, :, width:width + expert_count].astype(jnp.int32) - 1
    slots = slots.reshape(sources, tokens, rows_of_chips, halves)
    half = column // (COLUMNS // halves)
    slots = jnp.sum(jnp.where(jnp.arange(halves, dtype=jnp.int32) == half, slots, 0), axis=3)
    pieces = []
    for low, high in parts:
        place = jnp.arange(low, high, dtype=jnp.int32)
        match = slots.transpose(2, 0, 1)[:, None, None, :, :] == place[None, None, :, None, None]
        match = match & origin[None, :, None, :, None]
        pieces.append(match.reshape(rows_of_chips, sources * (high - low), sources * tokens))
    picker = jnp.concatenate(pieces, axis=1).astype(jnp.bfloat16)
    count = picker.shape[1]
    flat = everyone[:, :, :width].reshape(sources * tokens, width)
    packed = jnp.dot(picker.reshape(rows_of_chips * count, sources * tokens), flat, preferred_element_type=jnp.float32)
    packed = packed.astype(jnp.bfloat16).reshape(rows_of_chips, count, width)
    received = exchange_rows(packed)
    rows_in = []
    first = 0
    for low, high in parts:
        size = sources * (high - low)
        rows_in.append(received[:, first:first + size].reshape(rows_of_chips * size, width))
        first += size
    return jnp.concatenate(rows_in, axis=0)


def per_device(states, incoming, norm_gain, w_gate_up, w_down, routes, scores):
    group = lax.axis_size("expert") // SHARE
    copies = SLICES // SHARE
    expert_count = group // copies
    tokens = states.shape[1]
    capacity = min(tokens, max(2, 5 * tokens * TOPK // (4 * expert_count)))
    parts = []
    low = 0
    while low < capacity:
        high = min(low + ROWS, capacity)
        parts.append((low, high))
        low = high
    column = lax.axis_index("expert") % COLUMNS
    section_index = lax.axis_index("section")
    gate_up_own, down_own = w_gate_up[0, 0], w_down[0, 0]
    down_other = swapped(down_own)
    gate_up_other = swapped(gate_up_own)
    gain_values = norm_gain[0]
    plans = []
    for tick_index in range(TICKS):
        chosen = routes[tick_index, 0].reshape(-1)
        slot = slots_of(chosen, expert_count)
        router_scores = scores[tick_index, 0]
        weight = (router_scores / jnp.sum(router_scores, axis=-1, keepdims=True)).reshape(-1)
        plan = []
        for low, high in parts:
            size = high - low
            inside = (slot >= low) & (slot < high)
            target = jnp.where(inside, chosen * size + slot - low, -1)
            matches = jnp.arange(expert_count * size, dtype=jnp.int32)[:, None] == target[None, :]
            matches = matches.reshape(expert_count * size, tokens, TOPK)
            picker = jnp.any(matches, axis=2).astype(jnp.bfloat16)
            weights = jnp.sum(jnp.where(matches, weight.reshape(1, tokens, TOPK), 0.0), axis=2)
            upper = weights.astype(jnp.bfloat16)
            lower = (weights - upper.astype(jnp.float32)).astype(jnp.bfloat16)
            plan.append((picker, upper, lower))
        plans.append(plan)
    current = states[0]
    outputs = []
    for tick_index in range(TICKS):
        plan = plans[tick_index]
        normed = normalize(current, gain_values)
        at = [0]
        for low, high in parts:
            at.append(at[-1] + (high - low) * normed.shape[1] // LANES)
        if tick_index == 0:
            rows_in = first_dispatch(normed, routes[0, 0], parts, column, expert_count, down_other)
            rows_in, gate_up_other = lax.optimization_barrier((rows_in, gate_up_other))
        else:
            sent = []
            for (low, high), (picker, _, _) in zip(parts, plan):
                packed = jnp.dot(picker, normed, preferred_element_type=jnp.float32).astype(jnp.bfloat16)
                sent.append(to_tiles(packed, expert_count))
            received = exchange(jnp.repeat(jnp.concatenate(sent, axis=1), copies, axis=0))
            rows_in = [from_tiles(received[:, at[i]:at[i + 1]], high - low) for i, (low, high) in enumerate(parts)]
            rows_in = jnp.concatenate(rows_in, axis=0)
        hidden_own = gated(rows_in, gate_up_own)
        hidden_other = gated(rows_in, gate_up_other)
        partial_value = jnp.dot(hidden_own, down_own, preferred_element_type=jnp.float32)
        partial_value = partial_value + jnp.dot(hidden_other, down_other, preferred_element_type=jnp.float32)
        partial_value = partial_value.astype(jnp.bfloat16)
        split = [partial_value[group * low:group * high] for low, high in parts]
        back = exchange(jnp.concatenate([to_tiles(piece, group) for piece in split], axis=1))
        returned = [back[:, at[i]:at[i + 1]] for i in range(len(parts))]
        branch = 0.0
        for (low, high), piece, (_, upper, lower) in zip(parts, returned, plan):
            summed = jnp.sum(piece.reshape(expert_count, copies, piece.shape[1], LANES).astype(jnp.float32), axis=1)
            table = from_tiles(summed.astype(jnp.bfloat16), high - low)
            contract = (((0,), (0,)), ((), ()))
            branch = branch + lax.dot_general(upper, table, contract, preferred_element_type=jnp.float32)
            branch = branch + lax.dot_general(lower, table, contract, preferred_element_type=jnp.float32)
        result = (current.astype(jnp.float32) + branch).astype(jnp.bfloat16)
        outputs.append(result)
        if tick_index + 1 < TICKS:
            passed = shifted(result, "section", 1)
            current = jnp.where(section_index == 0, incoming[tick_index], passed)
    return jnp.stack(outputs)[:, None]


def solution(mesh):
    return jax.shard_map(
        per_device,
        mesh=mesh,
        in_specs=(
            P("section", "expert", None),
            P(None, "expert", None),
            P("section", None),
            P("section", "expert", None, None),
            P("section", "expert", None, None),
            P(None, "section", "expert", None),
            P(None, "section", "expert", None),
        ),
        out_specs=P(None, "section", "expert", None),
        check_vma=False,
    )
```

```python
import jax
import jax.numpy as jnp
from jax import lax
from jax.experimental import pallas as pl
from jax.experimental.pallas import tpu as pltpu
from jax.sharding import PartitionSpec as P

SLICES = 4
TOPK = 4
TICKS = 2
LANES = 128
ROWS = 8
COLUMNS = 8
SHARE = 2


epsilon = 1e-06


def shifted(x, axis, by):
    length = lax.axis_size(axis)
    pairs = [(i, i + by) for i in range(length) if 0 <= i + by < length]
    return lax.ppermute(x, axis, pairs)


def normalize(current, gain_values):
    values = current.astype(jnp.float32)
    mean_square = jnp.mean(values * values, axis=-1, keepdims=True)
    return (values * lax.rsqrt(mean_square + epsilon) * gain_values).astype(jnp.bfloat16)


def to_tiles(rows, groups):
    r = rows.shape[0] // groups
    blocks = rows.shape[1] // LANES
    return rows.reshape(groups, r, blocks, LANES).transpose(0, 2, 1, 3).reshape(groups, blocks * r, LANES)


def from_tiles(tiles, r):
    groups, _, _ = tiles.shape
    blocks = tiles.shape[1] // r
    return tiles.reshape(groups, blocks, r, LANES).transpose(0, 2, 1, 3).reshape(groups * r, blocks * LANES)


def slots_of(chosen, expert_count):
    onehot = (chosen[:, None] == jnp.arange(expert_count, dtype=jnp.int32)[None, :]).astype(jnp.int32)
    return jnp.sum((jnp.cumsum(onehot, axis=0) - onehot) * onehot, axis=1)


def exchange(x):
    length = lax.axis_size("expert")
    groups = [list(range(first, length, SHARE)) for first in range(SHARE)]
    return lax.all_to_all(x, "expert", split_axis=0, concat_axis=0, tiled=True, axis_index_groups=groups)


def same_side(x):
    length = lax.axis_size("expert")
    pieces = [x]
    for by in range(SHARE, COLUMNS, SHARE):
        pairs = [(i, i // COLUMNS * COLUMNS + (i + by) % COLUMNS) for i in range(length)]
        pieces.append(lax.ppermute(x, "expert", pairs))
    return jnp.stack(pieces)


def exchange_rows(x):
    length = lax.axis_size("expert")
    groups = [list(range(first, length, COLUMNS)) for first in range(COLUMNS)]
    return lax.all_to_all(x, "expert", split_axis=0, concat_axis=0, tiled=True, axis_index_groups=groups)


def swapped(x):
    length = lax.axis_size("expert")
    return lax.ppermute(x, "expert", [(i, i ^ 1) for i in range(length)])


def experts_kernel(slices, carried, x_ref, *refs):
    refs = list(refs)
    acc_ref = refs.pop(0) if carried else None
    gate_up = refs[:slices]
    down = refs[slices:2 * slices]
    out_ref, gate_up_buffer, down_buffer, total, gate_up_sems, down_sems = refs[2 * slices:]
    copies = []
    for i in range(slices):
        copies.append((
            pltpu.make_async_copy(gate_up[i], gate_up_buffer.at[i], gate_up_sems.at[i]),
            pltpu.make_async_copy(down[i], down_buffer.at[i], down_sems.at[i]),
        ))
    for first, second in copies:
        first.start()
        second.start()
    half = gate_up_buffer.shape[2] // 2
    for i, (first, second) in enumerate(copies):
        first.wait()
        projected = jnp.dot(x_ref[...], gate_up_buffer[i], preferred_element_type=jnp.float32)
        hidden = (jax.nn.silu(projected[:, :half]) * projected[:, half:]).astype(jnp.bfloat16)
        second.wait()
        value = jnp.dot(hidden, down_buffer[i], preferred_element_type=jnp.float32)
        if i > 0:
            value = total[...] + value
        elif carried:
            value = acc_ref[...] + value
        if i + 1 < slices:
            total[...] = value
        else:
            out_ref[...] = value.astype(out_ref.dtype)


def experts(rows, gate_up, down, carried=None, dtype=jnp.bfloat16):
    slices = len(gate_up)
    count, width = rows.shape
    out_width = down[0].shape[1]
    whole = pl.BlockSpec(memory_space=pltpu.VMEM)
    placed = pl.BlockSpec(memory_space=pl.ANY)
    operands = [rows] + ([] if carried is None else [carried]) + list(gate_up) + list(down)
    in_specs = [whole] * (1 if carried is None else 2) + [placed] * (2 * slices)
    body = lambda *refs: experts_kernel(slices, carried is not None, *refs)
    return pl.pallas_call(
        body,
        out_shape=jax.ShapeDtypeStruct((count, out_width), dtype),
        in_specs=in_specs,
        out_specs=whole,
        scratch_shapes=[
            pltpu.VMEM((slices,) + gate_up[0].shape, gate_up[0].dtype),
            pltpu.VMEM((slices,) + down[0].shape, down[0].dtype),
            pltpu.VMEM((count, out_width), jnp.float32),
            pltpu.SemaphoreType.DMA((slices,)),
            pltpu.SemaphoreType.DMA((slices,)),
        ],
        compiler_params=pltpu.CompilerParams(vmem_limit_bytes=32 << 20),
        name=f"experts_{slices}",
    )(*operands)


def first_dispatch(normed, chosen, parts, column, expert_count, swapped_first):
    tokens, width = normed.shape
    rows_of_chips = lax.axis_size("expert") // COLUMNS
    halves = expert_count // rows_of_chips
    sources = COLUMNS // SHARE
    slot = slots_of(chosen.reshape(-1), expert_count).reshape(tokens, TOPK)
    named = chosen[:, :, None] == jnp.arange(expert_count, dtype=jnp.int32)[None, None, :]
    slot_at = jnp.sum(jnp.where(named, slot[:, :, None] + 1, 0), axis=1)
    slot_at = jnp.pad(slot_at, ((0, 0), (0, LANES - expert_count))).astype(jnp.bfloat16)
    everyone = same_side(jnp.concatenate([normed, slot_at], axis=1))
    everyone, _ = lax.optimization_barrier((everyone, swapped_first))
    mine = column // SHARE
    position = (mine - jnp.arange(sources, dtype=jnp.int32)) % sources
    origin = jnp.arange(sources, dtype=jnp.int32)[:, None] == position[None, :]
    slots = everyone[:, :, width:width + expert_count].astype(jnp.int32) - 1
    slots = slots.reshape(sources, tokens, rows_of_chips, halves)
    half = column // (COLUMNS // halves)
    slots = jnp.sum(jnp.where(jnp.arange(halves, dtype=jnp.int32) == half, slots, 0), axis=3)
    pieces = []
    for low, high in parts:
        place = jnp.arange(low, high, dtype=jnp.int32)
        match = slots.transpose(2, 0, 1)[:, None, None, :, :] == place[None, None, :, None, None]
        match = match & origin[None, :, None, :, None]
        pieces.append(match.reshape(rows_of_chips, sources * (high - low), sources * tokens))
    picker = jnp.concatenate(pieces, axis=1).astype(jnp.bfloat16)
    count = picker.shape[1]
    flat = everyone[:, :, :width].reshape(sources * tokens, width)
    packed = jnp.dot(picker.reshape(rows_of_chips * count, sources * tokens), flat, preferred_element_type=jnp.float32)
    packed = packed.astype(jnp.bfloat16).reshape(rows_of_chips, count, width)
    received = exchange_rows(packed)
    rows_in = []
    first = 0
    for low, high in parts:
        size = sources * (high - low)
        rows_in.append(received[:, first:first + size].reshape(rows_of_chips * size, width))
        first += size
    return jnp.concatenate(rows_in, axis=0)


def per_device(states, incoming, norm_gain, w_gate_up, w_down, routes, scores):
    group = lax.axis_size("expert") // SHARE
    copies = SLICES // SHARE
    expert_count = group // copies
    tokens = states.shape[1]
    capacity = min(tokens, max(2, 5 * tokens * TOPK // (4 * expert_count)))
    parts = []
    low = 0
    while low < capacity:
        high = min(low + ROWS, capacity)
        parts.append((low, high))
        low = high
    column = lax.axis_index("expert") % COLUMNS
    section_index = lax.axis_index("section")
    gate_up_own, down_own = w_gate_up[0, 0], w_down[0, 0]
    down_other = swapped(down_own)
    gate_up_other = swapped(gate_up_own)
    gain_values = norm_gain[0]
    plans = []
    for tick_index in range(TICKS):
        chosen = routes[tick_index, 0].reshape(-1)
        slot = slots_of(chosen, expert_count)
        router_scores = scores[tick_index, 0]
        weight = (router_scores / jnp.sum(router_scores, axis=-1, keepdims=True)).reshape(-1)
        plan = []
        for low, high in parts:
            size = high - low
            inside = (slot >= low) & (slot < high)
            target = jnp.where(inside, chosen * size + slot - low, -1)
            matches = jnp.arange(expert_count * size, dtype=jnp.int32)[:, None] == target[None, :]
            matches = matches.reshape(expert_count * size, tokens, TOPK)
            picker = jnp.any(matches, axis=2).astype(jnp.bfloat16)
            weights = jnp.sum(jnp.where(matches, weight.reshape(1, tokens, TOPK), 0.0), axis=2)
            upper = weights.astype(jnp.bfloat16)
            lower = (weights - upper.astype(jnp.float32)).astype(jnp.bfloat16)
            plan.append((picker, upper, lower))
        plans.append(plan)
    current = states[0]
    outputs = []
    for tick_index in range(TICKS):
        plan = plans[tick_index]
        normed = normalize(current, gain_values)
        at = [0]
        for low, high in parts:
            at.append(at[-1] + (high - low) * normed.shape[1] // LANES)
        if tick_index == 0:
            rows_in = first_dispatch(normed, routes[0, 0], parts, column, expert_count, down_other)
            partial_value = experts(rows_in, [gate_up_own], [down_own], dtype=jnp.float32)
            rows_in, gate_up_other = lax.optimization_barrier((rows_in, gate_up_other))
            partial_value = experts(rows_in, [gate_up_other], [down_other], carried=partial_value)
        else:
            sent = []
            for (low, high), (picker, _, _) in zip(parts, plan):
                packed = jnp.dot(picker, normed, preferred_element_type=jnp.float32).astype(jnp.bfloat16)
                sent.append(to_tiles(packed, expert_count))
            received = exchange(jnp.repeat(jnp.concatenate(sent, axis=1), copies, axis=0))
            rows_in = [from_tiles(received[:, at[i]:at[i + 1]], high - low) for i, (low, high) in enumerate(parts)]
            rows_in = jnp.concatenate(rows_in, axis=0)
            partial_value = experts(rows_in, [gate_up_own, gate_up_other], [down_own, down_other])
        split = [partial_value[group * low:group * high] for low, high in parts]
        back = exchange(jnp.concatenate([to_tiles(piece, group) for piece in split], axis=1))
        returned = [back[:, at[i]:at[i + 1]] for i in range(len(parts))]
        branch = 0.0
        for (low, high), piece, (_, upper, lower) in zip(parts, returned, plan):
            summed = jnp.sum(piece.reshape(expert_count, copies, piece.shape[1], LANES).astype(jnp.float32), axis=1)
            table = from_tiles(summed.astype(jnp.bfloat16), high - low)
            contract = (((0,), (0,)), ((), ()))
            branch = branch + lax.dot_general(upper, table, contract, preferred_element_type=jnp.float32)
            branch = branch + lax.dot_general(lower, table, contract, preferred_element_type=jnp.float32)
        result = (current.astype(jnp.float32) + branch).astype(jnp.bfloat16)
        outputs.append(result)
        if tick_index + 1 < TICKS:
            passed = shifted(result, "section", 1)
            current = jnp.where(section_index == 0, incoming[tick_index], passed)
    return jnp.stack(outputs)[:, None]


def solution(mesh):
    return jax.shard_map(
        per_device,
        mesh=mesh,
        in_specs=(
            P("section", "expert", None),
            P(None, "expert", None),
            P("section", None),
            P("section", "expert", None, None),
            P("section", "expert", None, None),
            P(None, "section", "expert", None),
            P(None, "section", "expert", None),
        ),
        out_specs=P(None, "section", "expert", None),
        check_vma=False,
    )
```

```python
import jax
import jax.numpy as jnp
from jax import lax
from jax.sharding import PartitionSpec as P

SLICES = 4
TOPK = 4
TICKS = 2
LANES = 128
ROWS = 8
FAR = (3, 6, 5, 0, 7, 2, 1, 4)
NEAR = (7, 2, 1, 4, 3, 6, 5, 0)
COLUMNS = 8
SHARE = 2


epsilon = 1e-06


def shifted(x, axis, by):
    length = lax.axis_size(axis)
    pairs = [(i, i + by) for i in range(length) if 0 <= i + by < length]
    return lax.ppermute(x, axis, pairs)


def normalize(current, gain_values):
    values = current.astype(jnp.float32)
    mean_square = jnp.mean(values * values, axis=-1, keepdims=True)
    return (values * lax.rsqrt(mean_square + epsilon) * gain_values).astype(jnp.bfloat16)


def to_tiles(rows, groups):
    r = rows.shape[0] // groups
    blocks = rows.shape[1] // LANES
    return rows.reshape(groups, r, blocks, LANES).transpose(0, 2, 1, 3).reshape(groups, blocks * r, LANES)


def from_tiles(tiles, r):
    groups, _, _ = tiles.shape
    blocks = tiles.shape[1] // r
    return tiles.reshape(groups, blocks, r, LANES).transpose(0, 2, 1, 3).reshape(groups * r, blocks * LANES)


def slots_of(chosen, expert_count):
    onehot = (chosen[:, None] == jnp.arange(expert_count, dtype=jnp.int32)[None, :]).astype(jnp.int32)
    return jnp.sum((jnp.cumsum(onehot, axis=0) - onehot) * onehot, axis=1)


def side_of(column):
    return (column ^ (column >> 1)) % SHARE


def exchange(x):
    length = lax.axis_size("expert")
    groups = [[i for i in range(length) if side_of(i % COLUMNS) == side] for side in range(SHARE)]
    return lax.all_to_all(x, "expert", split_axis=0, concat_axis=0, tiled=True, axis_index_groups=groups)


def within_row(x, targets):
    length = lax.axis_size("expert")
    return lax.ppermute(x, "expert", [(i, i // COLUMNS * COLUMNS + targets[i % COLUMNS]) for i in range(length)])


def same_side(x):
    pair = jnp.stack([x, within_row(x, FAR)])
    return jnp.concatenate([pair, within_row(pair, NEAR)], axis=0)


def exchange_rows(x):
    length = lax.axis_size("expert")
    groups = [list(range(first, length, COLUMNS)) for first in range(COLUMNS)]
    return lax.all_to_all(x, "expert", split_axis=0, concat_axis=0, tiled=True, axis_index_groups=groups)


def swapped(x):
    length = lax.axis_size("expert")
    return lax.ppermute(x, "expert", [(i, i ^ 1) for i in range(length)])


def gated(rows, weights):
    half = weights.shape[1] // 2
    projected = jnp.dot(rows, weights, preferred_element_type=jnp.float32)
    return (jax.nn.silu(projected[:, :half]) * projected[:, half:]).astype(jnp.bfloat16)


def first_dispatch(normed, chosen, parts, column, expert_count, swapped_first):
    tokens, width = normed.shape
    rows_of_chips = lax.axis_size("expert") // COLUMNS
    halves = expert_count // rows_of_chips
    sources = COLUMNS // SHARE
    slot = slots_of(chosen.reshape(-1), expert_count).reshape(tokens, TOPK)
    named = chosen[:, :, None] == jnp.arange(expert_count, dtype=jnp.int32)[None, None, :]
    slot_at = jnp.sum(jnp.where(named, slot[:, :, None] + 1, 0), axis=1)
    slot_at = jnp.pad(slot_at, ((0, 0), (0, LANES - expert_count))).astype(jnp.bfloat16)
    everyone = same_side(jnp.concatenate([normed, slot_at], axis=1))
    everyone, _ = lax.optimization_barrier((everyone, swapped_first))
    arrivals = [[z, FAR[z], NEAR[z], FAR[NEAR[z]]] for z in range(COLUMNS)]
    position = jnp.asarray(arrivals, dtype=jnp.int32)[column] // SHARE
    origin = jnp.arange(sources, dtype=jnp.int32)[:, None] == position[None, :]
    slots = everyone[:, :, width:width + expert_count].astype(jnp.int32) - 1
    slots = slots.reshape(sources, tokens, rows_of_chips, halves)
    half = column // (COLUMNS // halves)
    slots = jnp.sum(jnp.where(jnp.arange(halves, dtype=jnp.int32) == half, slots, 0), axis=3)
    pieces = []
    for low, high in parts:
        place = jnp.arange(low, high, dtype=jnp.int32)
        match = slots.transpose(2, 0, 1)[:, None, None, :, :] == place[None, None, :, None, None]
        match = match & origin[None, :, None, :, None]
        pieces.append(match.reshape(rows_of_chips, sources * (high - low), sources * tokens))
    picker = jnp.concatenate(pieces, axis=1).astype(jnp.bfloat16)
    count = picker.shape[1]
    flat = everyone[:, :, :width].reshape(sources * tokens, width)
    packed = jnp.dot(picker.reshape(rows_of_chips * count, sources * tokens), flat, preferred_element_type=jnp.float32)
    packed = packed.astype(jnp.bfloat16).reshape(rows_of_chips, count, width)
    received = exchange_rows(packed)
    rows_in = []
    first = 0
    for low, high in parts:
        size = sources * (high - low)
        rows_in.append(received[:, first:first + size].reshape(rows_of_chips * size, width))
        first += size
    return jnp.concatenate(rows_in, axis=0)


def per_device(states, incoming, norm_gain, w_gate_up, w_down, routes, scores):
    group = lax.axis_size("expert") // SHARE
    copies = SLICES // SHARE
    expert_count = group // copies
    tokens = states.shape[1]
    capacity = min(tokens, max(2, 5 * tokens * TOPK // (4 * expert_count)))
    parts = []
    low = 0
    while low < capacity:
        high = min(low + ROWS, capacity)
        parts.append((low, high))
        low = high
    column = lax.axis_index("expert") % COLUMNS
    section_index = lax.axis_index("section")
    gate_up_own, down_own = w_gate_up[0, 0], w_down[0, 0]
    down_other = swapped(down_own)
    gate_up_other = swapped(gate_up_own)
    gain_values = norm_gain[0]
    plans = []
    for tick_index in range(TICKS):
        chosen = routes[tick_index, 0].reshape(-1)
        slot = slots_of(chosen, expert_count)
        router_scores = scores[tick_index, 0]
        weight = (router_scores / jnp.sum(router_scores, axis=-1, keepdims=True)).reshape(-1)
        plan = []
        for low, high in parts:
            size = high - low
            inside = (slot >= low) & (slot < high)
            target = jnp.where(inside, chosen * size + slot - low, -1)
            matches = jnp.arange(expert_count * size, dtype=jnp.int32)[:, None] == target[None, :]
            matches = matches.reshape(expert_count * size, tokens, TOPK)
            picker = jnp.any(matches, axis=2).astype(jnp.bfloat16)
            weights = jnp.sum(jnp.where(matches, weight.reshape(1, tokens, TOPK), 0.0), axis=2)
            upper = weights.astype(jnp.bfloat16)
            lower = (weights - upper.astype(jnp.float32)).astype(jnp.bfloat16)
            plan.append((picker, upper, lower))
        plans.append(plan)
    current = states[0]
    outputs = []
    for tick_index in range(TICKS):
        plan = plans[tick_index]
        normed = normalize(current, gain_values)
        at = [0]
        for low, high in parts:
            at.append(at[-1] + (high - low) * normed.shape[1] // LANES)
        if tick_index == 0:
            rows_in = first_dispatch(normed, routes[0, 0], parts, column, expert_count, down_other)
            rows_in, gate_up_other = lax.optimization_barrier((rows_in, gate_up_other))
        else:
            sent = []
            for (low, high), (picker, _, _) in zip(parts, plan):
                packed = jnp.dot(picker, normed, preferred_element_type=jnp.float32).astype(jnp.bfloat16)
                sent.append(to_tiles(packed, expert_count))
            received = exchange(jnp.repeat(jnp.concatenate(sent, axis=1), copies, axis=0))
            rows_in = [from_tiles(received[:, at[i]:at[i + 1]], high - low) for i, (low, high) in enumerate(parts)]
            rows_in = jnp.concatenate(rows_in, axis=0)
        hidden_own = gated(rows_in, gate_up_own)
        hidden_other = gated(rows_in, gate_up_other)
        partial_value = jnp.dot(hidden_own, down_own, preferred_element_type=jnp.float32)
        partial_value = partial_value + jnp.dot(hidden_other, down_other, preferred_element_type=jnp.float32)
        partial_value = partial_value.astype(jnp.bfloat16)
        split = [partial_value[group * low:group * high] for low, high in parts]
        back = exchange(jnp.concatenate([to_tiles(piece, group) for piece in split], axis=1))
        returned = [back[:, at[i]:at[i + 1]] for i in range(len(parts))]
        branch = 0.0
        for (low, high), piece, (_, upper, lower) in zip(parts, returned, plan):
            summed = jnp.sum(piece.reshape(expert_count, copies, piece.shape[1], LANES).astype(jnp.float32), axis=1)
            table = from_tiles(summed.astype(jnp.bfloat16), high - low)
            contract = (((0,), (0,)), ((), ()))
            branch = branch + lax.dot_general(upper, table, contract, preferred_element_type=jnp.float32)
            branch = branch + lax.dot_general(lower, table, contract, preferred_element_type=jnp.float32)
        result = (current.astype(jnp.float32) + branch).astype(jnp.bfloat16)
        outputs.append(result)
        if tick_index + 1 < TICKS:
            passed = shifted(result, "section", 1)
            current = jnp.where(section_index == 0, incoming[tick_index], passed)
    return jnp.stack(outputs)[:, None]


def solution(mesh):
    return jax.shard_map(
        per_device,
        mesh=mesh,
        in_specs=(
            P("section", "expert", None),
            P(None, "expert", None),
            P("section", None),
            P("section", "expert", None, None),
            P("section", "expert", None, None),
            P(None, "section", "expert", None),
            P(None, "section", "expert", None),
        ),
        out_specs=P(None, "section", "expert", None),
        check_vma=False,
    )
```

```python
import jax
import jax.numpy as jnp
from jax import lax
from jax.sharding import PartitionSpec as P

SLICES = 4
TOPK = 4
TICKS = 2
LANES = 128
ROWS = 8
FAR = (3, 6, 5, 0, 7, 2, 1, 4)
NEAR = (7, 2, 1, 4, 3, 6, 5, 0)
COLUMNS = 8
SHARE = 2


epsilon = 1e-06


def shifted(x, axis, by):
    length = lax.axis_size(axis)
    pairs = [(i, i + by) for i in range(length) if 0 <= i + by < length]
    return lax.ppermute(x, axis, pairs)


def normalize(current, gain_values):
    values = current.astype(jnp.float32)
    mean_square = jnp.mean(values * values, axis=-1, keepdims=True)
    return (values * lax.rsqrt(mean_square + epsilon) * gain_values).astype(jnp.bfloat16)


def to_tiles(rows, groups):
    r = rows.shape[0] // groups
    blocks = rows.shape[1] // LANES
    return rows.reshape(groups, r, blocks, LANES).transpose(0, 2, 1, 3).reshape(groups, blocks * r, LANES)


def from_tiles(tiles, r):
    groups, _, _ = tiles.shape
    blocks = tiles.shape[1] // r
    return tiles.reshape(groups, blocks, r, LANES).transpose(0, 2, 1, 3).reshape(groups * r, blocks * LANES)


def slots_of(chosen, expert_count):
    onehot = (chosen[:, None] == jnp.arange(expert_count, dtype=jnp.int32)[None, :]).astype(jnp.int32)
    return jnp.sum((jnp.cumsum(onehot, axis=0) - onehot) * onehot, axis=1)


def side_of(column):
    return (column ^ (column >> 1)) % SHARE


def exchange(x):
    length = lax.axis_size("expert")
    groups = [[i for i in range(length) if side_of(i % COLUMNS) == side] for side in range(SHARE)]
    return lax.all_to_all(x, "expert", split_axis=0, concat_axis=0, tiled=True, axis_index_groups=groups)


def within_row(x, targets):
    length = lax.axis_size("expert")
    return lax.ppermute(x, "expert", [(i, i // COLUMNS * COLUMNS + targets[i % COLUMNS]) for i in range(length)])


def same_side(x):
    pair = jnp.stack([x, within_row(x, FAR)])
    return jnp.concatenate([pair, within_row(pair, NEAR)], axis=0)


def exchange_rows(x):
    length = lax.axis_size("expert")
    groups = [list(range(first, length, COLUMNS)) for first in range(COLUMNS)]
    return lax.all_to_all(x, "expert", split_axis=0, concat_axis=0, tiled=True, axis_index_groups=groups)


def swapped(x):
    length = lax.axis_size("expert")
    return lax.ppermute(x, "expert", [(i, i ^ 1) for i in range(length)])


def gated(rows, weights):
    half = weights.shape[1] // 2
    projected = jnp.dot(rows, weights, preferred_element_type=jnp.float32)
    return (jax.nn.silu(projected[:, :half]) * projected[:, half:]).astype(jnp.bfloat16)


def first_dispatch(normed, chosen, parts, column, expert_count, swapped_first):
    tokens, width = normed.shape
    rows_of_chips = lax.axis_size("expert") // COLUMNS
    halves = expert_count // rows_of_chips
    sources = COLUMNS // SHARE
    slot = slots_of(chosen.reshape(-1), expert_count).reshape(tokens, TOPK)
    named = chosen[:, :, None] == jnp.arange(expert_count, dtype=jnp.int32)[None, None, :]
    slot_at = jnp.sum(jnp.where(named, slot[:, :, None] + 1, 0), axis=1)
    slot_at = jnp.pad(slot_at, ((0, 0), (0, LANES - expert_count))).astype(jnp.bfloat16)
    everyone = same_side(jnp.concatenate([normed, slot_at], axis=1))
    everyone, _ = lax.optimization_barrier((everyone, swapped_first))
    arrivals = [[z, FAR[z], NEAR[z], FAR[NEAR[z]]] for z in range(COLUMNS)]
    position = jnp.asarray(arrivals, dtype=jnp.int32)[column] // SHARE
    origin = jnp.arange(sources, dtype=jnp.int32)[:, None] == position[None, :]
    slots = everyone[:, :, width:width + expert_count].astype(jnp.int32) - 1
    slots = slots.reshape(sources, tokens, rows_of_chips, halves)
    half = column // (COLUMNS // halves)
    slots = jnp.sum(jnp.where(jnp.arange(halves, dtype=jnp.int32) == half, slots, 0), axis=3)
    pieces = []
    for low, high in parts:
        place = jnp.arange(low, high, dtype=jnp.int32)
        match = slots.transpose(2, 0, 1)[:, None, None, :, :] == place[None, None, :, None, None]
        match = match & origin[None, :, None, :, None]
        pieces.append(match.reshape(rows_of_chips, sources * (high - low), sources * tokens))
    picker = jnp.concatenate(pieces, axis=1).astype(jnp.bfloat16)
    count = picker.shape[1]
    flat = everyone[:, :, :width].reshape(sources * tokens, width)
    packed = jnp.dot(picker.reshape(rows_of_chips * count, sources * tokens), flat, preferred_element_type=jnp.float32)
    packed = packed.astype(jnp.bfloat16).reshape(rows_of_chips, count, width)
    received = exchange_rows(packed)
    rows_in = []
    first = 0
    for low, high in parts:
        size = sources * (high - low)
        rows_in.append(received[:, first:first + size].reshape(rows_of_chips * size, width))
        first += size
    return jnp.concatenate(rows_in, axis=0)


def per_device(states, incoming, norm_gain, w_gate_up, w_down, routes, scores):
    group = lax.axis_size("expert") // SHARE
    copies = SLICES // SHARE
    expert_count = group // copies
    tokens = states.shape[1]
    capacity = min(tokens, max(2, 5 * tokens * TOPK // (4 * expert_count)))
    parts = []
    low = 0
    while low < capacity:
        high = min(low + ROWS, capacity)
        parts.append((low, high))
        low = high
    column = lax.axis_index("expert") % COLUMNS
    section_index = lax.axis_index("section")
    gate_up_own, down_own = w_gate_up[0, 0], w_down[0, 0]
    early = down_own.shape[0] * 5 // 6
    down_early = down_own[:early]
    states, down_early = lax.optimization_barrier((states, down_early))
    down_early = swapped(down_early)
    down_late = swapped(down_own[early:])
    gate_up_other = swapped(gate_up_own)
    gain_values = norm_gain[0]
    plans = []
    for tick_index in range(TICKS):
        chosen = routes[tick_index, 0].reshape(-1)
        slot = slots_of(chosen, expert_count)
        router_scores = scores[tick_index, 0]
        weight = (router_scores / jnp.sum(router_scores, axis=-1, keepdims=True)).reshape(-1)
        plan = []
        for low, high in parts:
            size = high - low
            inside = (slot >= low) & (slot < high)
            target = jnp.where(inside, chosen * size + slot - low, -1)
            matches = jnp.arange(expert_count * size, dtype=jnp.int32)[:, None] == target[None, :]
            matches = matches.reshape(expert_count * size, tokens, TOPK)
            picker = jnp.any(matches, axis=2).astype(jnp.bfloat16)
            weights = jnp.sum(jnp.where(matches, weight.reshape(1, tokens, TOPK), 0.0), axis=2)
            upper = weights.astype(jnp.bfloat16)
            lower = (weights - upper.astype(jnp.float32)).astype(jnp.bfloat16)
            plan.append((picker, upper, lower))
        plans.append(plan)
    current = states[0]
    outputs = []
    for tick_index in range(TICKS):
        plan = plans[tick_index]
        normed = normalize(current, gain_values)
        at = [0]
        for low, high in parts:
            at.append(at[-1] + (high - low) * normed.shape[1] // LANES)
        if tick_index == 0:
            rows_in = first_dispatch(normed, routes[0, 0], parts, column, expert_count, down_early)
            rows_in, gate_up_other = lax.optimization_barrier((rows_in, gate_up_other))
        else:
            sent = []
            for (low, high), (picker, _, _) in zip(parts, plan):
                packed = jnp.dot(picker, normed, preferred_element_type=jnp.float32).astype(jnp.bfloat16)
                sent.append(to_tiles(packed, expert_count))
            received = exchange(jnp.repeat(jnp.concatenate(sent, axis=1), copies, axis=0))
            rows_in = [from_tiles(received[:, at[i]:at[i + 1]], high - low) for i, (low, high) in enumerate(parts)]
            rows_in = jnp.concatenate(rows_in, axis=0)
        hidden_own = gated(rows_in, gate_up_own)
        hidden_other = gated(rows_in, gate_up_other)
        partial_value = jnp.dot(hidden_own, down_own, preferred_element_type=jnp.float32)
        partial_value = partial_value + jnp.dot(hidden_other[:, :early], down_early, preferred_element_type=jnp.float32)
        partial_value = partial_value + jnp.dot(hidden_other[:, early:], down_late, preferred_element_type=jnp.float32)
        partial_value = partial_value.astype(jnp.bfloat16)
        split = [partial_value[group * low:group * high] for low, high in parts]
        back = exchange(jnp.concatenate([to_tiles(piece, group) for piece in split], axis=1))
        returned = [back[:, at[i]:at[i + 1]] for i in range(len(parts))]
        branch = 0.0
        for (low, high), piece, (_, upper, lower) in zip(parts, returned, plan):
            summed = jnp.sum(piece.reshape(expert_count, copies, piece.shape[1], LANES).astype(jnp.float32), axis=1)
            table = from_tiles(summed.astype(jnp.bfloat16), high - low)
            contract = (((0,), (0,)), ((), ()))
            branch = branch + lax.dot_general(upper, table, contract, preferred_element_type=jnp.float32)
            branch = branch + lax.dot_general(lower, table, contract, preferred_element_type=jnp.float32)
        result = (current.astype(jnp.float32) + branch).astype(jnp.bfloat16)
        outputs.append(result)
        if tick_index + 1 < TICKS:
            passed = shifted(result, "section", 1)
            current = jnp.where(section_index == 0, incoming[tick_index], passed)
    return jnp.stack(outputs)[:, None]


def solution(mesh):
    return jax.shard_map(
        per_device,
        mesh=mesh,
        in_specs=(
            P("section", "expert", None),
            P(None, "expert", None),
            P("section", None),
            P("section", "expert", None, None),
            P("section", "expert", None, None),
            P(None, "section", "expert", None),
            P(None, "section", "expert", None),
        ),
        out_specs=P(None, "section", "expert", None),
        check_vma=False,
    )
```
